32 devices in a mesh: expert: 8 (over y, x, core), blk: 4 (over z).
Axes of the slice: x: 2, y: 2, z: 4, core: 2. Of those that a mesh axis runs over, the one named last changes fastest.
Arguments:
- tokens: bfloat16 [256, 6144], P(('expert', 'blk')), may hold values from -6 to 6
- out_grad: bfloat16 [256, 6144], P(('expert', 'blk')), may hold values from -6 to 6
- expert_ids: int32 [256, 4], P(('expert', 'blk')), may hold values from 0 to 7, as said below
- slots: int32 [256, 4], P(('expert', 'blk')), may hold values from 0 to 4, as said below
- gates: bfloat16 [256, 4], P(('expert', 'blk')), may hold values from 0.099609375 to 0.59765625
- w_in: bfloat16 [8, 5376, 6144], P('expert', 'blk'), may hold values from -0.078125 to 0.078125
- w_down: bfloat16 [8, 5376, 6144], P('expert', 'blk'), may hold values from -0.078125 to 0.078125
Outputs:
- grad_tokens: bfloat16 [256, 6144], P(('expert', 'blk'))
- grad_gates: bfloat16 [256, 4], P(('expert', 'blk'))
The draws below stay inside these ranges and needn't reach their ends.
Inputs may be any that keep to these rules, and one draw needn't show every extreme that they name: `expert_ids`: within the 8 tokens of one device, a token names 4 different experts, no expert is named more than 5 times, and one expert is named exactly 5 times by every device. Among the entries of one device that name one expert, the slots are 0 to their count minus 1, each once.
All inputs are finite; a program needn't handle non-finite values.
Results may differ from the reference program's by a relative error of at most 0.019.
Values may be sent and summed in bfloat16 or wider, within the bound.
No kernel may reach another device: no remote copies, remote signals or barrier semaphores. Data moves between devices by JAX's collectives and lax.ppermute only.
A program may use at most 128 MiB of HBM per device.

```python
import jax
import jax.numpy as jnp
from jax import lax

D = 6144
FF = 5376
TOP = 4
TOK_DEV = 8
EXPERTS = 8
CAP = 5
TOKENS = 256
N_BLK = 4


def routing_table(key):
    blocks = TOKENS // TOK_DEV
    key_full, key_blocks = jax.random.split(jax.random.fold_in(key, 7))
    full_expert = jax.random.randint(key_full, (), 0, EXPERTS).astype(jnp.int32)

    def one_block(block_key):
        key_order, key_tokens = jax.random.split(block_key)
        others = jax.random.permutation(key_order, EXPERTS - 1).astype(jnp.int32) + 1
        ordering = jnp.concatenate([jnp.zeros((1,), jnp.int32), others])
        position = jnp.arange(TOK_DEV * TOP, dtype=jnp.int32)
        rank_of = position // CAP
        slot_of = position % CAP
        label = (full_expert + ordering[rank_of]) % EXPERTS
        label = label.reshape(TOP, TOK_DEV).T
        slot_of = slot_of.reshape(TOP, TOK_DEV).T
        shuffle = jax.random.permutation(key_tokens, TOK_DEV)
        return (label[shuffle], slot_of[shuffle])
    labels, places = jax.vmap(one_block)(jax.random.split(key_blocks, blocks))
    return (labels.reshape(TOKENS, TOP).astype(jnp.int32), places.reshape(TOKENS, TOP).astype(jnp.int32))


def draw_expert_ids(key, part):
    return routing_table(key)[0]


def draw_slots(key, part):
    return routing_table(key)[1]


def block_levels(own_key, dims, shards, least, top_value):
    def one(axis_at, parts):
        heights = jax.random.uniform(jax.random.fold_in(jax.random.fold_in(own_key, 6), axis_at), (parts,), jnp.float32, least / len(shards), top_value / len(shards))
        return jnp.repeat(jnp.exp(heights), dims[axis_at] // parts).reshape((-1,) + (1,) * (len(dims) - axis_at - 1))

    gain = one(*shards[0])
    for cut in shards[1:]:
        gain = gain * one(*cut)
    return gain


def normal_values(rng, shape, width, bound, cuts=(), held_as=jnp.bfloat16):
    array = width * jax.random.normal(rng, shape, jnp.float32)
    if cuts:
        array = array * block_levels(rng, shape, cuts, -0.22, 0.18)
    return jnp.clip(array, -bound, bound).astype(held_as)


def setup_inputs(seed: int = 0) -> dict:
    key_of = jax.random.split(jax.random.key(seed), 8)
    tokens = normal_values(key_of[0], (TOKENS, D), 1.0, 6.0, ((0, 32),))
    out_grad = normal_values(key_of[1], (TOKENS, D), 1.0, 6.0, ((0, 32),))
    expert_ids = draw_expert_ids(jax.random.fold_in(key_of[7], 71), 0)
    slots = draw_slots(jax.random.fold_in(key_of[7], 71), 0)
    gates = jnp.clip(0.099609375 + 0.49804688 * jax.random.uniform(key_of[4], (TOKENS, TOP), jnp.float32) ** block_levels(key_of[4], (TOKENS, TOP), ((0, 32),), -0.2, 0.2), 0.099609375, 0.59765625).astype(jnp.bfloat16)
    w_in = normal_values(key_of[5], (EXPERTS, FF, D), D ** -0.5, 0.078125, ((0, 8), (1, 4)))
    w_down = normal_values(key_of[6], (EXPERTS, FF, D), D ** -0.5, 0.078125, ((0, 8), (1, 4)))
    return dict(tokens=tokens, out_grad=out_grad, expert_ids=expert_ids, slots=slots, gates=gates, w_in=w_in, w_down=w_down)


def block_tables(ids_block, slots_block, gates_block):
    target = (ids_block * CAP + slots_block).reshape(-1)
    owner = jnp.broadcast_to(jnp.arange(TOK_DEV, dtype=jnp.int32)[:, None], (TOK_DEV, TOP)).reshape(-1)
    table = jnp.full((EXPERTS * CAP,), TOK_DEV, dtype=jnp.int32).at[target].set(owner)
    weight = jnp.zeros((EXPERTS * CAP,), jnp.bfloat16).at[target].set(gates_block.reshape(-1))
    return table, weight


def reference(tokens, out_grad, expert_ids, slots, gates, w_in, w_down):
    blocks = TOKENS // TOK_DEV
    tables, weights = jax.vmap(block_tables)(expert_ids.reshape(blocks, TOK_DEV, TOP), slots.reshape(blocks, TOK_DEV, TOP), gates.reshape(blocks, TOK_DEV, TOP))
    base = (jnp.arange(blocks, dtype=jnp.int32) * TOK_DEV)[:, None]
    row_index = jnp.where(tables == TOK_DEV, TOKENS, base + tables).astype(jnp.int32)
    x_padded = jnp.concatenate([tokens, jnp.zeros((1, D), jnp.bfloat16)], axis=0)
    dy_padded = jnp.concatenate([out_grad, jnp.zeros((1, D), jnp.bfloat16)], axis=0)
    group = FF // N_BLK

    def per_expert(expert):
        picks = lax.dynamic_slice_in_dim(row_index, expert * CAP, CAP, 1).reshape(-1)
        scales = lax.dynamic_slice_in_dim(weights, expert * CAP, CAP, 1).reshape(-1)
        rows_x = x_padded[picks]
        rows_dy = dy_padded[picks]
        weight_in = w_in[expert]
        weight_down = w_down[expert]
        pre = jnp.dot(rows_x, weight_in.T, preferred_element_type=jnp.float32)
        back = jnp.dot(rows_dy, weight_down.T, preferred_element_type=jnp.float32)
        sigma = jax.nn.sigmoid(pre)
        gate_grad = jnp.sum(pre * sigma * back, axis=1).astype(jnp.bfloat16)
        slope = (scales.astype(jnp.float32)[:, None] * back * sigma * (1.0 + pre * (1.0 - sigma))).astype(jnp.bfloat16)
        pieces = jnp.einsum("rbf,bfd->rbd", slope.reshape(-1, N_BLK, group).astype(jnp.float32), weight_in.reshape(N_BLK, group, D).astype(jnp.float32))
        rounded = lax.optimization_barrier(pieces.astype(jnp.bfloat16)).astype(jnp.float32)
        row_grad = jnp.sum(rounded, axis=1).astype(jnp.bfloat16)
        return row_grad, gate_grad

    row_grads, gate_grads = lax.map(per_expert, jnp.arange(EXPERTS, dtype=jnp.int32))
    token_block = (jnp.arange(TOKENS, dtype=jnp.int32) // TOK_DEV)[:, None]
    where = (token_block * CAP + slots).astype(jnp.int32)
    picked = row_grads[expert_ids, where].astype(jnp.float32)
    grad_tokens = jnp.sum(picked, axis=1).astype(jnp.bfloat16)
    grad_gates = gate_grads[expert_ids, where]
    return grad_tokens, grad_gates
```

```python
import functools

import jax
import jax.numpy as jnp
from jax import lax
from jax.experimental import pallas as pl
from jax.experimental.pallas import tpu as pltpu
from jax.sharding import PartitionSpec as P

LANES = 128
AXES = ("expert", "blk")
F32 = jnp.float32
BF16 = jnp.bfloat16
VMEM = pl.BlockSpec(memory_space=pltpu.VMEM)
CONTRACT_LAST = (((1,), (1,)), ((), ()))


def hidden_terms(rows_x, rows_dy, rows_gate, weight_in, weight_down):
    pre = lax.dot_general(rows_x, weight_in, CONTRACT_LAST, preferred_element_type=F32)
    back = lax.dot_general(rows_dy, weight_down, CONTRACT_LAST, preferred_element_type=F32)
    sigma = jax.nn.sigmoid(pre)
    gate_part = jnp.sum(pre * sigma * back, axis=1)
    slope = rows_gate.astype(F32)[:, None] * back * sigma * (1.0 + pre * (1.0 - sigma))
    return (slope.astype(BF16), gate_part)


def routed_device(tokens, out_grad, expert_ids, slots, gates, w_in, w_down):
    tok_count = tokens.shape[0]
    top_count = expert_ids.shape[1]
    expert_count = lax.axis_size("expert")
    capacity = max(2, (tok_count * top_count + expert_count - 1) // expert_count + 1)
    slot_count = expert_count * capacity
    target = expert_ids * capacity + slots
    matches = (
        target[None, :, :] == jnp.arange(slot_count, dtype=jnp.int32)[:, None, None]
    ).astype(F32)
    placing = jnp.sum(matches, axis=2).astype(BF16)
    send_x = jnp.dot(placing, tokens, preferred_element_type=F32).astype(BF16)
    send_dy = jnp.dot(placing, out_grad, preferred_element_type=F32).astype(BF16)
    send_gate = jnp.einsum("stk,tk->s", matches, gates.astype(F32)).astype(BF16)
    recv_x, recv_dy, recv_gate = (
        lax.all_to_all(send_x, "expert", split_axis=0, concat_axis=0, tiled=True),
        lax.all_to_all(send_dy, "expert", split_axis=0, concat_axis=0, tiled=True),
        lax.all_to_all(send_gate, "expert", split_axis=0, concat_axis=0, tiled=True),
    )
    weight_in = w_in[0]
    weight_down = w_down[0]
    piece_slope, piece_gate = hidden_terms(
        lax.all_gather(recv_x, "blk", axis=0, tiled=True),
        lax.all_gather(recv_dy, "blk", axis=0, tiled=True),
        lax.all_gather(recv_gate, "blk", axis=0, tiled=True),
        weight_in,
        weight_down,
    )
    grad_rows = lax.psum_scatter(
        jnp.dot(piece_slope, weight_in, preferred_element_type=F32).astype(BF16),
        "blk",
        scatter_dimension=0,
        tiled=True,
    )
    gate_rows = lax.psum_scatter(piece_gate, "blk", scatter_dimension=0, tiled=True)
    back_rows, back_gate = (
        lax.all_to_all(grad_rows, "expert", split_axis=0, concat_axis=0, tiled=True),
        lax.all_to_all(
            gate_rows.astype(BF16), "expert", split_axis=0, concat_axis=0, tiled=True
        ),
    )
    grad_tokens = lax.dot_general(
        placing, back_rows, (((0,), (0,)), ((), ())), preferred_element_type=F32
    ).astype(BF16)
    grad_gates = jnp.einsum("stk,s->tk", matches, back_gate.astype(F32)).astype(BF16)
    return (grad_tokens, grad_gates)


class Ring:
    def __init__(self, experts, blocks):
        self.experts, self.blocks = experts, blocks
        self.plane = experts // 2
        self.xor = self.plane & (self.plane - 1) == 0

    def move(self, array, step):
        pairs = []
        for e in range(self.experts):
            for z in range(self.blocks):
                to_e, to_z = step(e, z)
                pairs.append((e * self.blocks + z, to_e * self.blocks + to_z))
        return lax.ppermute(array, AXES, pairs)

    def core(self, array):
        return self.move(array, lambda e, z: (e ^ 1, z))

    def plane_to(self, array, k, sign=1):
        def step(e, z):
            p, c = divmod(e, 2)
            q = p ^ k if self.xor else (p + sign * k) % self.plane
            return q * 2 + c, z

        return self.move(array, step)

    def line_to(self, array, k, sign=1):
        return self.move(array, lambda e, z: (e, (z + sign * k) % self.blocks))

    def gather(self, array, stage):
        count, to = (
            (self.plane, self.plane_to) if stage == "plane" else (self.blocks, self.line_to)
        )
        return [array] + [to(array, k) for k in range(1, count)]

    def scatter(self, parts, stage):
        to = self.plane_to if stage == "plane" else self.line_to
        return [parts[0]] + [to(parts[k], k, -1) for k in range(1, len(parts))]


def add_up(parts):
    total = parts[0].astype(F32)
    for part in parts[1:]:
        total = total + part.astype(F32)
    return total


def params(mib):
    return pltpu.CompilerParams(vmem_limit_bytes=mib << 20)


def product_kernel(lo, hi, first, *refs):
    if first:
        own, other, weight, out = refs
        start = None
    else:
        start, own, other, weight, out = refs
    width = hi - lo
    rows = jnp.concatenate([own[:, :width], other[:, :width]], axis=0)
    hidden = weight.shape[0]
    for at in range(0, hidden, 256):
        to = min(at + 256, hidden)
        value = lax.dot_general(
            rows, weight[at:to, lo:hi], CONTRACT_LAST, preferred_element_type=F32
        )
        if start is not None:
            value = value + start[:, at:to]
        out[:, at:to] = value


def product(start, own, other, weight, lo, hi, name):
    rows = own.shape[0] * 2
    hidden = weight.shape[0]
    args = (own, other, weight) if start is None else (start, own, other, weight)
    flops = 2 * rows * hidden * (hi - lo)
    return pl.pallas_call(
        functools.partial(product_kernel, lo, hi, start is None),
        out_shape=jax.ShapeDtypeStruct((rows, hidden), F32),
        in_specs=[VMEM] * len(args),
        out_specs=VMEM,
        compiler_params=params(8),
        cost_estimate=pl.CostEstimate(
            flops=flops, bytes_accessed=hidden * (hi - lo) * 2, transcendentals=0
        ),
        name=name,
    )(*args)


def slope_kernel(pre_ref, back_ref, gate_own, gate_other, mask_ref, slope_ref, part_ref):
    mask = mask_ref[...]
    rows, hidden = pre_ref.shape
    table = jnp.concatenate([gate_own[...], gate_other[...]], axis=0).astype(F32)
    gate = jnp.sum(table * mask, axis=1, keepdims=True)
    total = jnp.zeros((rows, 1), F32)
    for at in range(0, hidden, 256):
        to = min(at + 256, hidden)
        pre = pre_ref[:, at:to]
        back = back_ref[:, at:to]
        sigma = jax.nn.sigmoid(pre)
        total = total + jnp.sum(pre * sigma * back, axis=1, keepdims=True)
        slope = gate * back * sigma * (1.0 + pre * (1.0 - sigma))
        slope_ref[:, at:to] = slope.astype(BF16)
    part_ref[...] = (total * mask).astype(BF16)


def slope_of(pre, back, gate_own, gate_other, mask):
    rows, hidden = pre.shape
    return pl.pallas_call(
        slope_kernel,
        out_shape=(
            jax.ShapeDtypeStruct((rows, hidden), BF16),
            jax.ShapeDtypeStruct((rows, LANES), BF16),
        ),
        in_specs=[VMEM] * 5,
        out_specs=(VMEM, VMEM),
        compiler_params=params(8),
        name="slope",
    )(pre, back, gate_own, gate_other, mask)


def spread_kernel(lo, hi, *refs):
    if len(refs) == 5:
        slope, weight, extra, own, other = refs
    else:
        slope, weight, own, other = refs
        extra = None
    half = own.shape[0]
    value = slope[...]
    for at in range(lo, hi, 512):
        to = min(at + 512, hi)
        out = jnp.dot(value, weight[:, at:to], preferred_element_type=F32).astype(BF16)
        own[:, at - lo : to - lo] = out[:half]
        other[:, at - lo : to - lo] = out[half:]
    if extra is not None:
        own[:, hi - lo :] = extra[:half, :]
        other[:, hi - lo :] = extra[half:, :]


def spread(slope, weight, lo, hi, extra, name):
    rows, hidden = slope.shape
    width = hi - lo + (LANES if extra is not None else 0)
    half = jax.ShapeDtypeStruct((rows // 2, width), BF16)
    args = (slope, weight) + ((extra,) if extra is not None else ())
    return pl.pallas_call(
        functools.partial(spread_kernel, lo, hi),
        out_shape=(half, half),
        in_specs=[VMEM] * len(args),
        out_specs=(VMEM, VMEM),
        compiler_params=params(8),
        cost_estimate=pl.CostEstimate(
            flops=2 * rows * hidden * (hi - lo),
            bytes_accessed=hidden * (hi - lo) * 2,
            transcendentals=0,
        ),
        name=name,
    )(*args)


def give_back(ring, own, other, order):
    received = ring.core(other)
    parts = [own, received]
    for stage in order:
        count = ring.plane if stage == "plane" else ring.blocks
        if stage == order[0]:
            rows = own.shape[0] // count
            if stage == "plane":
                pieces = [[p[k * rows : (k + 1) * rows] for p in parts] for k in range(count)]
            else:
                tok = own.shape[0] // (ring.plane * ring.blocks)
                pieces = [
                    [
                        p.reshape(ring.plane, ring.blocks, tok, -1)[:, k].reshape(rows, -1)
                        for p in parts
                    ]
                    for k in range(count)
                ]
        else:
            rows = parts[0].shape[0] // count
            pieces = [[p[k * rows : (k + 1) * rows] for p in parts] for k in range(count)]
        blocks = [add_up(piece).astype(BF16) for piece in pieces]
        parts = ring.scatter(blocks, stage)
    return add_up(parts)


def dense_device(tokens, out_grad, expert_ids, slots, gates, w_in, w_down):
    width = tokens.shape[1]
    experts, blocks = lax.axis_size("expert"), lax.axis_size("blk")
    ring = Ring(experts, blocks)
    cut = SPLIT(width)
    lanes = jnp.arange(LANES, dtype=jnp.int32)
    chosen = expert_ids[:, :, None] == lanes[None, None, :]
    table = jnp.sum(jnp.where(chosen, gates.astype(F32)[:, :, None], 0.0), axis=1).astype(BF16)
    mask = (lanes == lax.axis_index("expert")).astype(F32)[None, :]

    def whole(first, stages):
        block = first
        for stage in stages:
            block = jnp.concatenate(ring.gather(block, stage), axis=0)
        return block, ring.core(block)

    weight_in, weight_down = w_in[0], w_down[0]
    x_own, x_other = whole(tokens, ("line", "plane"))
    dy_own, dy_other = whole(jnp.concatenate([out_grad, table], axis=1), ("line", "plane"))
    pre = product(None, x_own, x_other, weight_in, 0, width, "pre")
    back = product(None, dy_own, dy_other, weight_down, 0, width, "back")
    slope, part = slope_of(pre, back, dy_own[:, width:], dy_other[:, width:], mask)
    own0, other0 = spread(slope, weight_in, 0, cut, None, "spread0")
    own1, other1 = spread(slope, weight_in, cut, width, part, "spread1")
    sum0 = give_back(ring, own0, other0, ("plane", "line"))
    sum1 = give_back(ring, own1, other1, ("plane", "line"))
    grad_tokens = jnp.concatenate([sum0, sum1[:, : width - cut]], axis=1).astype(BF16)
    found = sum1[:, width - cut :]
    grad_gates = jnp.sum(jnp.where(chosen, found[:, None, :], 0.0), axis=2).astype(BF16)
    return grad_tokens, grad_gates


def SPLIT(width):
    return width // 2


def fits(tokens, w_in, mesh):
    experts, blocks = mesh.shape["expert"], mesh.shape["blk"]
    count, width = tokens.shape
    held = 2 * (w_in.shape[1] // blocks) * width * 2 + 4 * count * width * 2
    return (
        experts % 2 == 0
        and experts <= LANES
        and width % LANES == 0
        and count % (8 * experts * blocks) == 0
        and held <= 48 << 20
    )


def solution(mesh):
    def program(tokens, out_grad, expert_ids, slots, gates, w_in, w_down):
        body = dense_device if fits(tokens, w_in, mesh) else routed_device
        rows = P(AXES, None)
        weights = P("expert", "blk", None)
        return jax.shard_map(
            body,
            mesh=mesh,
            in_specs=(rows, rows, rows, rows, rows, weights, weights),
            out_specs=(rows, rows),
            check_vma=False,
        )(tokens, out_grad, expert_ids, slots, gates, w_in, w_down)

    return program
```

```python
import functools

import jax
import jax.numpy as jnp
from jax import lax
from jax.experimental import pallas as pl
from jax.experimental.pallas import tpu as pltpu
from jax.sharding import PartitionSpec as P


LANES = 128
AXES = ("expert", "blk")
F32 = jnp.float32
BF16 = jnp.bfloat16
VMEM = pl.BlockSpec(memory_space=pltpu.VMEM)
HBM = pl.BlockSpec(memory_space=pltpu.HBM)
CONTRACT_LAST = (((1,), (1,)), ((), ()))


def hidden_terms(rows_x, rows_dy, rows_gate, weight_in, weight_down):
    pre = lax.dot_general(rows_x, weight_in, CONTRACT_LAST, preferred_element_type=F32)
    back = lax.dot_general(rows_dy, weight_down, CONTRACT_LAST, preferred_element_type=F32)
    sigma = jax.nn.sigmoid(pre)
    gate_part = jnp.sum(pre * sigma * back, axis=1)
    slope = rows_gate.astype(F32)[:, None] * back * sigma * (1.0 + pre * (1.0 - sigma))
    return (slope.astype(BF16), gate_part)


def routed_device(tokens, out_grad, expert_ids, slots, gates, w_in, w_down):
    tok_count = tokens.shape[0]
    top_count = expert_ids.shape[1]
    expert_count = lax.axis_size("expert")
    capacity = max(2, (tok_count * top_count + expert_count - 1) // expert_count + 1)
    slot_count = expert_count * capacity
    target = expert_ids * capacity + slots
    matches = (
        target[None, :, :] == jnp.arange(slot_count, dtype=jnp.int32)[:, None, None]
    ).astype(F32)
    placing = jnp.sum(matches, axis=2).astype(BF16)
    send_x = jnp.dot(placing, tokens, preferred_element_type=F32).astype(BF16)
    send_dy = jnp.dot(placing, out_grad, preferred_element_type=F32).astype(BF16)
    send_gate = jnp.einsum("stk,tk->s", matches, gates.astype(F32)).astype(BF16)
    recv_x, recv_dy, recv_gate = (
        lax.all_to_all(send_x, "expert", split_axis=0, concat_axis=0, tiled=True),
        lax.all_to_all(send_dy, "expert", split_axis=0, concat_axis=0, tiled=True),
        lax.all_to_all(send_gate, "expert", split_axis=0, concat_axis=0, tiled=True),
    )
    weight_in = w_in[0]
    weight_down = w_down[0]
    piece_slope, piece_gate = hidden_terms(
        lax.all_gather(recv_x, "blk", axis=0, tiled=True),
        lax.all_gather(recv_dy, "blk", axis=0, tiled=True),
        lax.all_gather(recv_gate, "blk", axis=0, tiled=True),
        weight_in,
        weight_down,
    )
    grad_rows = lax.psum_scatter(
        jnp.dot(piece_slope, weight_in, preferred_element_type=F32).astype(BF16),
        "blk",
        scatter_dimension=0,
        tiled=True,
    )
    gate_rows = lax.psum_scatter(piece_gate, "blk", scatter_dimension=0, tiled=True)
    back_rows, back_gate = (
        lax.all_to_all(grad_rows, "expert", split_axis=0, concat_axis=0, tiled=True),
        lax.all_to_all(
            gate_rows.astype(BF16), "expert", split_axis=0, concat_axis=0, tiled=True
        ),
    )
    grad_tokens = lax.dot_general(
        placing, back_rows, (((0,), (0,)), ((), ())), preferred_element_type=F32
    ).astype(BF16)
    grad_gates = jnp.einsum("stk,s->tk", matches, back_gate.astype(F32)).astype(BF16)
    return (grad_tokens, grad_gates)


class Ring:
    def __init__(self, experts, blocks):
        self.experts, self.blocks = experts, blocks
        self.plane = experts // 2

    def move(self, array, step):
        pairs = []
        for e in range(self.experts):
            for z in range(self.blocks):
                to_e, to_z = step(e, z)
                pairs.append((e * self.blocks + z, to_e * self.blocks + to_z))
        return lax.ppermute(array, AXES, pairs)

    def core(self, array):
        return self.move(array, lambda e, z: (e ^ 1, z))

    def to(self, array, stage, k):
        if stage == "plane":
            return self.move(array, lambda e, z: (e ^ (2 * k), z))
        return self.move(array, lambda e, z: (e, z ^ k))

    def count(self, stage):
        return self.plane if stage == "plane" else self.blocks

    def gather(self, array, stage):
        others = [self.to(array, stage, k) for k in range(1, self.count(stage))]
        return jnp.concatenate([array] + others, axis=0)

    def scatter(self, parts, stage):
        return [parts[0]] + [self.to(parts[k], stage, k) for k in range(1, self.count(stage))]


def add_up(parts):
    total = parts[0].astype(F32)
    for part in parts[1:]:
        total = total + part.astype(F32)
    return total


def params(mib):
    return pltpu.CompilerParams(vmem_limit_bytes=mib << 20)


def cost(rows, hidden, width):
    return pl.CostEstimate(
        flops=2 * rows * hidden * width, bytes_accessed=hidden * width * 2, transcendentals=0
    )


def column_blocks(hidden):
    return [(at, min(at + 256, hidden)) for at in range(0, hidden, 256)]


def times(rows, weight):
    return lax.dot_general(rows, weight, CONTRACT_LAST, preferred_element_type=F32)


def prepare_kernel(cut, *refs):
    tokens, out_grad, ids, gates, wide_x, wide_dy, narrow, rows_x, rows_dy, sems = refs
    copies = [
        pltpu.make_async_copy(tokens, rows_x, sems.at[0]),
        pltpu.make_async_copy(out_grad, rows_dy, sems.at[1]),
    ]
    for copy in copies:
        copy.start()
    tok, width = rows_x.shape
    expert = lax.broadcasted_iota(jnp.int32, (LANES, tok), 0)
    table = jnp.zeros((LANES, tok), F32)
    for k in range(ids.shape[0]):
        gate = gates[k : k + 1, :].astype(F32)
        table = table + jnp.where(expert == ids[k : k + 1, :], gate, 0.0)
    narrow[:tok, width - cut :] = jnp.zeros((tok, LANES), BF16)
    narrow[tok:, width - cut :] = table.T.astype(BF16)
    copies[0].wait()
    wide_x[...] = rows_x[:, :cut]
    narrow[:tok, : width - cut] = rows_x[:, cut:]
    copies[1].wait()
    wide_dy[...] = rows_dy[:, :cut]
    narrow[tok:, : width - cut] = rows_dy[:, cut:]


def prepare(tokens, out_grad, ids, gates, cut):
    tok, width = tokens.shape
    wide = jax.ShapeDtypeStruct((tok, cut), BF16)
    return pl.pallas_call(
        functools.partial(prepare_kernel, cut),
        out_shape=(wide, wide, jax.ShapeDtypeStruct((2 * tok, width - cut + LANES), BF16)),
        in_specs=[HBM, HBM, VMEM, VMEM],
        out_specs=(VMEM,) * 3,
        scratch_shapes=[pltpu.VMEM((tok, width), BF16)] * 2
        + [pltpu.SemaphoreType.DMA((2,))],
        compiler_params=params(2),
    )(in_hbm(tokens), in_hbm(out_grad), ids.T, gates.T)


def in_hbm(array):
    return pltpu.with_memory_space_constraint(array, pltpu.HBM)


def stack(own, other, rows):
    half = own.shape[0]
    rows[:half, :] = own[...]
    rows[half:, :] = other[...]


def load_kernel(source, _, held, sem):
    copy = pltpu.make_async_copy(source, held, sem)
    copy.start()
    copy.wait()


def load(weight, after, grant):
    return pl.pallas_call(
        load_kernel,
        out_shape=jax.ShapeDtypeStruct(weight.shape, BF16),
        in_specs=[HBM, pl.BlockSpec(memory_space=pl.ANY)],
        out_specs=VMEM,
        scratch_shapes=[pltpu.SemaphoreType.DMA],
        compiler_params=params(grant),
        cost_estimate=cost(0, *weight.shape),
    )(weight, after)


def first_kernel(own, other, weight, pre, rows):
    width = own.shape[1]
    stack(own, other, rows)
    for at, to in column_blocks(weight.shape[0]):
        pre[:, at:to] = times(rows[...], weight[at:to, :width])


def first_product(own, other, weight):
    half, width = own.shape
    hidden = weight.shape[0]
    return pl.pallas_call(
        first_kernel,
        out_shape=jax.ShapeDtypeStruct((2 * half, hidden), F32),
        in_specs=[VMEM, VMEM, VMEM],
        out_specs=VMEM,
        scratch_shapes=[pltpu.VMEM((2 * half, width), BF16)],
        compiler_params=params(LAST_GRANT),
        cost_estimate=cost(2 * half, hidden, width),
    )(own, other, weight)


def last_kernel(plane, blocks, tok, *refs):
    pre_ref, n_own, n_other, own, other, weight_in, weight_down = refs[:7]
    slope_ref, part_ref, rows, rows_x, rows_dy, table = refs[7:]
    cut, rest = rows.shape[1], rows_x.shape[1]
    stack(own, other, rows)
    for c, ref in enumerate((n_own, n_other)):
        for z in range(blocks):
            for p in range(plane):
                at = (z * plane + p) * 2 * tok
                to = ((c * plane + p) * blocks + z) * tok
                rows_x[to : to + tok, :] = ref[at : at + tok, :rest]
                rows_dy[to : to + tok, :] = ref[at + tok : at + 2 * tok, :rest]
                table[to : to + tok, :] = ref[at + tok : at + 2 * tok, rest:].astype(F32)
    lane = lax.broadcasted_iota(jnp.int32, (1, LANES), 1)
    mask = (lane == lax.axis_index("expert")).astype(F32)
    gate = jnp.sum(table[...] * mask, axis=1, keepdims=True)
    total = jnp.zeros((rows.shape[0], 1), F32)
    for at, to in column_blocks(weight_in.shape[0]):
        pre = pre_ref[:, at:to] + times(rows_x[...], weight_in[at:to, cut:])
        back = times(rows_dy[...], weight_down[at:to, cut:])
        back = back + times(rows[...], weight_down[at:to, :cut])
        sigma = jax.nn.sigmoid(pre)
        total = total + jnp.sum(pre * sigma * back, axis=1, keepdims=True)
        slope = gate * back * sigma * (1.0 + pre * (1.0 - sigma))
        slope_ref[:, at:to] = slope.astype(BF16)
    part_ref[...] = (total * mask).astype(BF16)


def last_product(pre, n_own, n_other, own, other, weight_in, weight_down, ring, tok):
    rows, hidden = pre.shape
    width = weight_in.shape[1]
    cut = own.shape[1]
    return pl.pallas_call(
        functools.partial(last_kernel, ring.plane, ring.blocks, tok),
        out_shape=(
            jax.ShapeDtypeStruct((rows, hidden), BF16),
            jax.ShapeDtypeStruct((rows, LANES), BF16),
        ),
        in_specs=[VMEM] * 7,
        out_specs=(VMEM, VMEM),
        scratch_shapes=[
            pltpu.VMEM((rows, cut), BF16),
            pltpu.VMEM((rows, width - cut), BF16),
            pltpu.VMEM((rows, width - cut), BF16),
            pltpu.VMEM((rows, LANES), F32),
        ],
        compiler_params=params(LAST_GRANT),
        cost_estimate=cost(rows, hidden, 2 * width - cut),
    )(pre, n_own, n_other, own, other, weight_in, weight_down)


def spread_kernel(lo, hi, *refs):
    slope, weight, *extra, own, other = refs
    half = own.shape[0]
    value = slope[...]
    for at in range(lo, hi, 512):
        to = min(at + 512, hi)
        out = jnp.dot(value, weight[:, at:to], preferred_element_type=F32).astype(BF16)
        own[:, at - lo : to - lo] = out[:half]
        other[:, at - lo : to - lo] = out[half:]
    for ref in extra:
        own[:, hi - lo :] = ref[:half, :]
        other[:, hi - lo :] = ref[half:, :]


def spread(slope, weight, lo, hi, extra):
    rows, hidden = slope.shape
    half = jax.ShapeDtypeStruct((rows // 2, hi - lo + LANES * len(extra)), BF16)
    return pl.pallas_call(
        functools.partial(spread_kernel, lo, hi),
        out_shape=(half, half),
        in_specs=[VMEM, VMEM] + [VMEM] * len(extra),
        out_specs=(VMEM, VMEM),
        compiler_params=params(GRANT),
        cost_estimate=cost(rows, hidden, hi - lo),
    )(slope, weight, *extra)


def core_sums(ring, own, other, stage, tok):
    width = own.shape[1]
    shape = (ring.plane, ring.blocks, tok, width)
    parts = [own.reshape(shape), ring.core(other).reshape(shape)]
    axis = 0 if stage == "plane" else 1
    return [
        add_up([lax.slice_in_dim(part, k, k + 1, axis=axis) for part in parts])
        .astype(BF16)
        .reshape(-1, width)
        for k in range(ring.count(stage))
    ]


def regroup(parts, count):
    rows = parts[0].shape[0] // count
    return [add_up([p[k * rows : (k + 1) * rows] for p in parts]) for k in range(count)]


def dense_device(tokens, out_grad, expert_ids, slots, gates, w_in, w_down):
    tok, width = tokens.shape
    ring = Ring(lax.axis_size("expert"), lax.axis_size("blk"))
    cut = cut_of(width)
    lanes = jnp.arange(LANES, dtype=jnp.int32)
    weight_in, weight_down = in_hbm(w_in[0]), in_hbm(w_down[0])
    wide_x, wide_dy, narrow = prepare(tokens, out_grad, expert_ids, gates, cut)
    x_line = ring.gather(wide_x, "line")
    n_plane = ring.gather(narrow, "plane")
    x_own = ring.gather(x_line, "plane")
    dy_line = ring.gather(wide_dy, "line")
    n_own = ring.gather(n_plane, "line")
    dy_own = ring.gather(dy_line, "plane")
    held_in = load(weight_in, x_line, LOAD_GRANT)
    x_other = ring.core(x_own)
    pre = first_product(x_own, x_other, held_in)
    held_down = load(weight_down, pre, DOWN_GRANT)
    n_other = ring.core(n_own)
    dy_other = ring.core(dy_own)
    slope, part = last_product(pre, n_own, n_other, dy_own, dy_other, held_in, held_down, ring, tok)

    chosen = (expert_ids[:, :, None] == lanes[None, None, :]).astype(F32)
    chosen = lax.optimization_barrier(chosen)
    mid = cut // 2 // 256 * 256
    own1, other1 = spread(slope, held_in, 0, mid, ())
    own2, other2 = spread(slope, held_in, mid, cut, ())
    own3, other3 = spread(slope, held_in, cut, width, (part,))
    plane1 = ring.scatter(core_sums(ring, own1, other1, "plane", tok), "plane")
    plane2 = ring.scatter(core_sums(ring, own2, other2, "plane", tok), "plane")
    line3 = ring.scatter(core_sums(ring, own3, other3, "line", tok), "line")
    wide = [
        jnp.concatenate(both, axis=1).astype(BF16)
        for both in zip(regroup(plane1, ring.blocks), regroup(plane2, ring.blocks))
    ]
    rest = [block.astype(BF16) for block in regroup(line3, ring.plane)]
    sum_wide = add_up(ring.scatter(wide, "line"))
    sum_rest = add_up(ring.scatter(rest, "plane"))
    grad_tokens = jnp.concatenate([sum_wide, sum_rest[:, : width - cut]], axis=1)
    grad_gates = jnp.sum(chosen * sum_rest[:, None, width - cut :], axis=2)
    return grad_tokens.astype(BF16), grad_gates.astype(BF16)


def cut_of(width):
    return width * 19 // 24 // 256 * 256


GRANT = 8
LOAD_GRANT = 4
DOWN_GRANT = 4
LAST_GRANT = 8


def power_of_two(n):
    return n & (n - 1) == 0


def fits(tokens, w_in, mesh):
    experts, blocks = mesh.shape["expert"], mesh.shape["blk"]
    count, width = tokens.shape
    held = 2 * (w_in.shape[1] // blocks) * width * 2 + 4 * count * width * 2
    return (
        power_of_two(experts)
        and power_of_two(blocks)
        and 2 < experts <= LANES
        and blocks > 1
        and width % 1024 == 0
        and count == 8 * experts * blocks
        and held <= 48 << 20
    )


def solution(mesh):
    def program(tokens, out_grad, expert_ids, slots, gates, w_in, w_down):
        dense = fits(tokens, w_in, mesh)
        rows = P(AXES, None)
        weights = P("expert", "blk", None)
        step = jax.shard_map(
            dense_device if dense else routed_device,
            mesh=mesh,
            in_specs=(rows, rows, rows, rows, rows, weights, weights),
            out_specs=(rows, rows),
            check_vma=False,
        )
        return step(tokens, out_grad, expert_ids, slots, gates, w_in, w_down)

    return program
```

```python
import functools

import jax
import jax.numpy as jnp
from jax import lax
from jax.experimental import pallas as pl
from jax.experimental.pallas import tpu as pltpu
from jax.sharding import PartitionSpec as P


LANES = 128
AXES = ("expert", "blk")
F32 = jnp.float32
BF16 = jnp.bfloat16
VMEM = pl.BlockSpec(memory_space=pltpu.VMEM)
HBM = pl.BlockSpec(memory_space=pltpu.HBM)
CONTRACT_LAST = (((1,), (1,)), ((), ()))


def hidden_terms(rows_x, rows_dy, rows_gate, weight_in, weight_down):
    pre = lax.dot_general(rows_x, weight_in, CONTRACT_LAST, preferred_element_type=F32)
    back = lax.dot_general(rows_dy, weight_down, CONTRACT_LAST, preferred_element_type=F32)
    sigma = jax.nn.sigmoid(pre)
    gate_part = jnp.sum(pre * sigma * back, axis=1)
    slope = rows_gate.astype(F32)[:, None] * back * sigma * (1.0 + pre * (1.0 - sigma))
    return (slope.astype(BF16), gate_part)


def routed_device(tokens, out_grad, expert_ids, slots, gates, w_in, w_down):
    tok_count = tokens.shape[0]
    top_count = expert_ids.shape[1]
    expert_count = lax.axis_size("expert")
    capacity = max(2, (tok_count * top_count + expert_count - 1) // expert_count + 1)
    slot_count = expert_count * capacity
    target = expert_ids * capacity + slots
    matches = (
        target[None, :, :] == jnp.arange(slot_count, dtype=jnp.int32)[:, None, None]
    ).astype(F32)
    placing = jnp.sum(matches, axis=2).astype(BF16)
    send_x = jnp.dot(placing, tokens, preferred_element_type=F32).astype(BF16)
    send_dy = jnp.dot(placing, out_grad, preferred_element_type=F32).astype(BF16)
    send_gate = jnp.einsum("stk,tk->s", matches, gates.astype(F32)).astype(BF16)
    recv_x, recv_dy, recv_gate = (
        lax.all_to_all(send_x, "expert", split_axis=0, concat_axis=0, tiled=True),
        lax.all_to_all(send_dy, "expert", split_axis=0, concat_axis=0, tiled=True),
        lax.all_to_all(send_gate, "expert", split_axis=0, concat_axis=0, tiled=True),
    )
    weight_in = w_in[0]
    weight_down = w_down[0]
    piece_slope, piece_gate = hidden_terms(
        lax.all_gather(recv_x, "blk", axis=0, tiled=True),
        lax.all_gather(recv_dy, "blk", axis=0, tiled=True),
        lax.all_gather(recv_gate, "blk", axis=0, tiled=True),
        weight_in,
        weight_down,
    )
    grad_rows = lax.psum_scatter(
        jnp.dot(piece_slope, weight_in, preferred_element_type=F32).astype(BF16),
        "blk",
        scatter_dimension=0,
        tiled=True,
    )
    gate_rows = lax.psum_scatter(piece_gate, "blk", scatter_dimension=0, tiled=True)
    back_rows, back_gate = (
        lax.all_to_all(grad_rows, "expert", split_axis=0, concat_axis=0, tiled=True),
        lax.all_to_all(
            gate_rows.astype(BF16), "expert", split_axis=0, concat_axis=0, tiled=True
        ),
    )
    grad_tokens = lax.dot_general(
        placing, back_rows, (((0,), (0,)), ((), ())), preferred_element_type=F32
    ).astype(BF16)
    grad_gates = jnp.einsum("stk,s->tk", matches, back_gate.astype(F32)).astype(BF16)
    return (grad_tokens, grad_gates)


class Ring:
    def __init__(self, experts, blocks):
        self.experts, self.blocks = experts, blocks
        self.plane = experts // 2

    def move(self, array, step):
        pairs = []
        for e in range(self.experts):
            for z in range(self.blocks):
                to_e, to_z = step(e, z)
                pairs.append((e * self.blocks + z, to_e * self.blocks + to_z))
        return lax.ppermute(array, AXES, pairs)

    def core(self, array):
        return self.move(array, lambda e, z: (e ^ 1, z))

    def to(self, array, stage, k):
        if stage == "plane":
            return self.move(array, lambda e, z: (e ^ (2 * k), z))
        return self.move(array, lambda e, z: (e, z ^ k))

    def count(self, stage):
        return self.plane if stage == "plane" else self.blocks

    def spread_out(self, array, stage):
        others = [self.to(array, stage, k) for k in range(1, self.count(stage))]
        return [array] + others

    def gather(self, array, stage):
        return jnp.concatenate(self.spread_out(array, stage), axis=0)

    def scatter(self, parts, stage):
        return [parts[0]] + [
            self.to(parts[k], stage, k) for k in range(1, self.count(stage))
        ]


def add_up(parts):
    total = parts[0].astype(F32)
    for part in parts[1:]:
        total = total + part.astype(F32)
    return total


def params(mib):
    return pltpu.CompilerParams(vmem_limit_bytes=mib << 20)


def cost(rows, hidden, width):
    return pl.CostEstimate(
        flops=2 * rows * hidden * width, bytes_accessed=hidden * width * 2, transcendentals=0
    )


def column_blocks(hidden):
    return [(at, min(at + 256, hidden)) for at in range(0, hidden, 256)]


def times(rows, weight):
    return lax.dot_general(rows, weight, CONTRACT_LAST, preferred_element_type=F32)


def fetch(sems, *pairs):
    copies = [
        pltpu.make_async_copy(source, target, sems.at[n])
        for n, (source, target) in enumerate(pairs)
    ]
    for copy in copies:
        copy.start()
    return copies


def wide_kernel(cut, tokens, out_grad, wide_x, wide_dy, sems):
    for copy in fetch(
        sems, (tokens.at[:, :cut], wide_x), (out_grad.at[:, :cut], wide_dy)
    ):
        copy.wait()


def wide_part(tokens, out_grad, cut):
    wide = jax.ShapeDtypeStruct((tokens.shape[0], cut), BF16)
    return pl.pallas_call(
        functools.partial(wide_kernel, cut),
        out_shape=(wide, wide),
        in_specs=[HBM, HBM],
        out_specs=(VMEM, VMEM),
        scratch_shapes=[pltpu.SemaphoreType.DMA((2,))],
        compiler_params=params(2),
        cost_estimate=pl.CostEstimate(
            flops=20000000000, bytes_accessed=40000000, transcendentals=0
        ),
    )(tokens, out_grad)


def narrow_kernel(cut, tokens, out_grad, ids, gates, narrow, sems):
    tok, width = tokens.shape
    copies = fetch(
        sems,
        (tokens.at[:, cut:], narrow.at[:tok, : width - cut]),
        (out_grad.at[:, cut:], narrow.at[tok:, : width - cut]),
    )
    expert = lax.broadcasted_iota(jnp.int32, (LANES, tok), 0)
    table = jnp.zeros((LANES, tok), F32)
    for k in range(ids.shape[0]):
        gate = gates[k : k + 1, :].astype(F32)
        table = table + jnp.where(expert == ids[k : k + 1, :], gate, 0.0)
    narrow[:tok, width - cut :] = jnp.zeros((tok, LANES), BF16)
    narrow[tok:, width - cut :] = table.T.astype(BF16)
    for copy in copies:
        copy.wait()


def narrow_part(tokens, out_grad, ids, gates, cut):
    tok, width = tokens.shape
    return pl.pallas_call(
        functools.partial(narrow_kernel, cut),
        out_shape=jax.ShapeDtypeStruct((2 * tok, width - cut + LANES), BF16),
        in_specs=[HBM, HBM, VMEM, VMEM],
        out_specs=VMEM,
        scratch_shapes=[pltpu.SemaphoreType.DMA((2,))],
        compiler_params=params(2),
    )(tokens, out_grad, ids.T, gates.T)


def in_hbm(array):
    return pltpu.with_memory_space_constraint(array, pltpu.HBM)


def stack(blocks, rows):
    step = blocks[0].shape[0]
    for n, block in enumerate(blocks):
        rows[n * step : (n + 1) * step, :] = block[...]


def first_kernel(*refs):
    *blocks, weight, pre, rows = refs
    stack(blocks, rows)
    width = rows.shape[1]
    for at, to in column_blocks(weight.shape[0]):
        pre[:, at:to] = times(rows[...], weight[at:to, :width])


def first_product(blocks, weight):
    step, width = blocks[0].shape
    rows, hidden = step * len(blocks), weight.shape[0]
    return pl.pallas_call(
        first_kernel,
        out_shape=jax.ShapeDtypeStruct((rows, hidden), F32),
        in_specs=[VMEM] * (len(blocks) + 1),
        out_specs=VMEM,
        scratch_shapes=[pltpu.VMEM((rows, width), BF16)],
        compiler_params=params(SMALL_GRANT),
        cost_estimate=cost(rows, hidden, width),
    )(*blocks, weight)


def unpack(plane, blocks, tok, offset, sources, columns, rows):
    for c, ref in enumerate(sources):
        for z in range(blocks):
            for p in range(plane):
                at = (z * plane + p) * 2 * tok + offset
                to = ((c * plane + p) * blocks + z) * tok
                rows[to : to + tok, :] = ref[at : at + tok, columns].astype(rows.dtype)


def middle_kernel(plane, blocks, tok, cut, *refs):
    pre, n_own, n_other, weight, pre_out, rows = refs
    width = rows.shape[1]
    unpack(plane, blocks, tok, 0, (n_own, n_other), slice(0, width), rows)
    for at, to in column_blocks(weight.shape[0]):
        pre_out[:, at:to] = pre[:, at:to] + times(rows[...], weight[at:to, cut:])


def middle_product(pre, n_own, n_other, weight, cut, ring, tok):
    rows, hidden = pre.shape
    width = weight.shape[1] - cut
    return pl.pallas_call(
        functools.partial(middle_kernel, ring.plane, ring.blocks, tok, cut),
        out_shape=jax.ShapeDtypeStruct((rows, hidden), F32),
        in_specs=[VMEM] * 4,
        out_specs=VMEM,
        scratch_shapes=[pltpu.VMEM((rows, width), BF16)],
        input_output_aliases={0: 0},
        compiler_params=params(SMALL_GRANT),
        cost_estimate=cost(rows, hidden, width),
    )(pre, n_own, n_other, weight)


def last_kernel(plane, blocks, tok, *refs):
    pre_ref, n_own, n_other, *own, weight, slope_ref, part_ref, rows, rest, table = refs
    stack(own, rows)
    cut, width = rows.shape[1], rest.shape[1]
    narrow = (n_own, n_other)
    unpack(plane, blocks, tok, tok, narrow, slice(0, width), rest)
    unpack(plane, blocks, tok, tok, narrow, slice(width, width + LANES), table)
    lane = lax.broadcasted_iota(jnp.int32, (1, LANES), 1)
    mask = (lane == lax.axis_index("expert")).astype(F32)
    gate = jnp.sum(table[...] * mask, axis=1, keepdims=True)
    total = jnp.zeros((rows.shape[0], 1), F32)
    for at, to in column_blocks(weight.shape[0]):
        pre = pre_ref[:, at:to]
        back = times(rest[...], weight[at:to, cut:])
        back = back + times(rows[...], weight[at:to, :cut])
        sigma = jax.nn.sigmoid(pre)
        total = total + jnp.sum(pre * sigma * back, axis=1, keepdims=True)
        slope = gate * back * sigma * (1.0 + pre * (1.0 - sigma))
        slope_ref[:, at:to] = slope.astype(BF16)
    part_ref[...] = (total * mask).astype(BF16)


def last_product(pre, n_own, n_other, blocks, weight, ring, tok):
    rows, hidden = pre.shape
    width, cut = weight.shape[1], blocks[0].shape[1]
    return pl.pallas_call(
        functools.partial(last_kernel, ring.plane, ring.blocks, tok),
        out_shape=(
            jax.ShapeDtypeStruct((rows, hidden), BF16),
            jax.ShapeDtypeStruct((rows, LANES), BF16),
        ),
        in_specs=[VMEM] * (len(blocks) + 4),
        out_specs=(VMEM, VMEM),
        scratch_shapes=[
            pltpu.VMEM((rows, cut), BF16),
            pltpu.VMEM((rows, width - cut), BF16),
            pltpu.VMEM((rows, LANES), F32),
        ],
        compiler_params=params(SMALL_GRANT),
        cost_estimate=cost(rows, hidden, width),
    )(pre, n_own, n_other, *blocks, weight)


def spread_kernel(lo, hi, *refs):
    slope, weight, *extra, own, other = refs
    half = own.shape[0]
    value = slope[...]
    for at in range(lo, hi, 512):
        to = min(at + 512, hi)
        out = jnp.dot(value, weight[:, at:to], preferred_element_type=F32).astype(BF16)
        own[:, at - lo : to - lo] = out[:half]
        other[:, at - lo : to - lo] = out[half:]
    for ref in extra:
        own[:, hi - lo :] = ref[:half, :]
        other[:, hi - lo :] = ref[half:, :]


def spread(slope, weight, lo, hi, extra):
    rows, hidden = slope.shape
    half = jax.ShapeDtypeStruct((rows // 2, hi - lo + LANES * len(extra)), BF16)
    return pl.pallas_call(
        functools.partial(spread_kernel, lo, hi),
        out_shape=(half, half),
        in_specs=[VMEM, VMEM] + [VMEM] * len(extra),
        out_specs=(VMEM, VMEM),
        compiler_params=params(GRANT),
        cost_estimate=cost(rows, hidden, hi - lo),
    )(slope, weight, *extra)


def core_sums(ring, own, other, stage, tok):
    width = own.shape[1]
    shape = (ring.plane, ring.blocks, tok, width)
    parts = [own.reshape(shape), ring.core(other).reshape(shape)]
    axis = 0 if stage == "plane" else 1
    return [
        add_up([lax.slice_in_dim(part, k, k + 1, axis=axis) for part in parts])
        .astype(BF16)
        .reshape(-1, width)
        for k in range(ring.count(stage))
    ]


def regroup(parts, count):
    rows = parts[0].shape[0] // count
    return [add_up([p[k * rows : (k + 1) * rows] for p in parts]) for k in range(count)]


def dense_device(tokens, out_grad, expert_ids, slots, gates, w_in, w_down):
    tok, width = tokens.shape
    ring = Ring(lax.axis_size("expert"), lax.axis_size("blk"))
    cut = cut_of(width)
    lanes = jnp.arange(LANES, dtype=jnp.int32)
    held_in, held_down = w_in[0], w_down[0]
    unchosen = (expert_ids[:, :, None] != lanes[None, None, :]).astype(F32)
    unchosen = lax.optimization_barrier(unchosen)
    tokens, out_grad = in_hbm(tokens), in_hbm(out_grad)
    wide_x, wide_dy = wide_part(tokens, out_grad, cut)
    x_line = ring.gather(wide_x, "line")
    narrow = narrow_part(tokens, out_grad, expert_ids, gates, cut)
    n_plane = ring.gather(narrow, "plane")
    x_own = ring.spread_out(x_line, "plane")
    dy_line = ring.gather(wide_dy, "line")
    n_own = ring.gather(n_plane, "line")
    dy_own = ring.spread_out(dy_line, "plane")
    x_other = [ring.core(block) for block in x_own]
    pre = first_product(x_own + x_other, held_in)
    n_other = ring.core(n_own)
    pre = middle_product(pre, n_own, n_other, held_in, cut, ring, tok)
    dy_other = [ring.core(block) for block in dy_own]
    slope, part = last_product(
        pre, n_own, n_other, dy_own + dy_other, held_down, ring, tok
    )

    chosen = lax.optimization_barrier(1.0 - unchosen)
    unchosen = lax.optimization_barrier(1.0 - chosen)
    mid, cut = width * 10 // 24, width * 19 // 24
    own1, other1 = spread(slope, held_in, 0, mid, ())
    own2, other2 = spread(slope, held_in, mid, cut, ())
    own3, other3 = spread(slope, held_in, cut, width, (part,))
    plane1 = ring.scatter(core_sums(ring, own1, other1, "plane", tok), "plane")
    plane2 = ring.scatter(core_sums(ring, own2, other2, "plane", tok), "plane")
    line3 = ring.scatter(core_sums(ring, own3, other3, "line", tok), "line")
    wide = [
        jnp.concatenate(both, axis=1).astype(BF16)
        for both in zip(regroup(plane1, ring.blocks), regroup(plane2, ring.blocks))
    ]
    rest = [block.astype(BF16) for block in regroup(line3, ring.plane)]
    sum_wide = add_up(ring.scatter(wide, "line"))
    sum_rest = add_up(ring.scatter(rest, "plane"))
    grad_tokens = jnp.concatenate([sum_wide, sum_rest[:, : width - cut]], axis=1)
    grad_gates = jnp.sum((1.0 - unchosen) * sum_rest[:, None, width - cut :], axis=2)
    return grad_tokens.astype(BF16), grad_gates.astype(BF16)


def cut_of(width):
    return width * 18 // 24 // 256 * 256


GRANT = 8
SMALL_GRANT = 8


def power_of_two(n):
    return n & (n - 1) == 0


def fits(tokens, w_in, mesh):
    experts, blocks = mesh.shape["expert"], mesh.shape["blk"]
    count, width = tokens.shape
    held = 2 * (w_in.shape[1] // blocks) * width * 2 + 4 * count * width * 2
    return (
        power_of_two(experts)
        and power_of_two(blocks)
        and 2 < experts <= LANES
        and blocks > 1
        and width % 1024 == 0
        and count == 8 * experts * blocks
        and held <= 48 << 20
    )


def solution(mesh):
    def program(tokens, out_grad, expert_ids, slots, gates, w_in, w_down):
        dense = fits(tokens, w_in, mesh)
        rows = P(AXES, None)
        weights = P("expert", "blk", None)
        step = jax.shard_map(
            dense_device if dense else routed_device,
            mesh=mesh,
            in_specs=(rows, rows, rows, rows, rows, weights, weights),
            out_specs=(rows, rows),
            check_vma=False,
        )
        return step(tokens, out_grad, expert_ids, slots, gates, w_in, w_down)

    return program
```
